32 devices in a mesh: groups: 2 (over y), srv: 4 (over z), hid: 2 (over x), rep: 2 (over core).
Axes of the slice: x: 2, y: 2, z: 4, core: 2. Of those that a mesh axis runs over, the one named last changes fastest.
Arguments:
- layer_input: bfloat16 [2048, 4096], P(('groups', 'srv'), ('hid', 'rep')), parts along dimension 0, may hold values from -12 to 12
- query_weight: bfloat16 [4096, 4096], P('srv', ('hid', 'rep')), may hold values from -0.09375 to 0.09375
- key_weight: bfloat16 [4096, 1024], P('srv', ('hid', 'rep')), may hold values from -0.09375 to 0.09375
- value_weight: bfloat16 [4096, 1024], P('srv', ('hid', 'rep')), may hold values from -0.09375 to 0.09375
- out_grad: bfloat16 [2048, 4096], P(('groups', 'srv'), ('hid', 'rep')), parts along dimension 0, may hold values from -6 to 6
- doc_ids: int32 [2048], P('groups'), parts along dimension 0, may hold values from 0 to 7, never falling along the last dimension, each value on 1 to 512 neighbouring positions
Outputs:
- input_grad: bfloat16 [2048, 4096], P(('groups', 'srv'), ('hid', 'rep')), parts along dimension 0
- query_weight_grad: float32 [8192, 4096], P(('groups', 'srv'), ('hid', 'rep')), parts along dimension 0
- key_weight_grad: float32 [8192, 1024], P(('groups', 'srv'), ('hid', 'rep')), parts along dimension 0
- value_weight_grad: float32 [8192, 1024], P(('groups', 'srv'), ('hid', 'rep')), parts along dimension 0
The draws below stay inside these ranges and needn't reach their ends.
There are 2 independent parts, one for each index of `groups`. The reference program is written for one: setup_inputs(seed, part) draws one part's arguments, and reference() takes and returns one part's arrays. A program takes and returns all parts, laid end to end along the dimension named above; an argument that names none is the same for every part. Nothing has to cross between parts.
Inputs may be any that keep to these rules, and one draw needn't show every extreme that they name: `doc_ids`: document numbers never fall along the tokens; every document holds at most 512 tokens and one holds exactly 512.
All inputs are finite; a program needn't handle non-finite values.
Results may differ from the reference program's by a relative error of at most 0.011.
Values may be sent and summed in bfloat16 or wider, within the bound.
A program may use at most 64 MiB of HBM per device.

```python
import math
import jax
import jax.numpy as jnp
import numpy as np
from jax import lax

D = 4096
HQ = 32
HK = 8
DH = 128
DOCS = 8
TOKENS = 1024
MAXDOC = 512


def draw_layer_input(key, part):
    values_drawn = jax.random.normal(jax.random.fold_in(key, 11), (TOKENS, D), jnp.float32)
    values_drawn = jnp.clip(values_drawn, -6.0, 6.0)
    return values_drawn.astype(jnp.bfloat16)


def block_levels(rng, extent, cuts, smallest, largest):
    factor_of = 1.0
    for dim, shards_of in cuts:
        heights = jax.random.uniform(jax.random.fold_in(jax.random.fold_in(rng, 6), dim), (shards_of,), jnp.float32, smallest / len(cuts), largest / len(cuts))
        factor_of = factor_of * jnp.repeat(jnp.exp(heights), extent[dim] // shards_of).reshape((-1,) + (1,) * (len(extent) - 1 - dim))
    return factor_of


def length_profile(count, total, limit, skew):
    weights = [(1 << 20) // math.isqrt(rank ** skew) + 1 for rank in range(2, count + 1)]
    spare, holding = total - limit - (count - 1), [1] * (count - 1)
    while spare > 0:
        movable = [i for i in range(count - 1) if holding[i] < limit]
        whole, remaining = sum([weights[i] for i in movable]), spare
        for i in movable:
            more = min(limit - holding[i], max(1, remaining * weights[i] // whole), spare)
            holding[i] = holding[i] + more
            spare = spare - more
    return np.array([limit] + holding)


def uneven_parts(own_key, number_of, total, limit, skew):
    if number_of == 2:
        one = jax.random.randint(own_key, (), max(1, total - limit), min(limit, total - 1) + 1)
        return jnp.stack([one, total - one])
    sizes = jnp.asarray(length_profile(number_of, total, limit, skew), jnp.int32)
    pairs = (number_of - 1) // 2
    giver, sink = sizes[1:1 + 2 * pairs:2], sizes[2:2 + 2 * pairs:2]
    margin = jnp.minimum(giver - 1, limit - sink)
    shifted = jax.random.randint(jax.random.fold_in(own_key, 1), (pairs,), 0, 1 << 20) % (margin + 1)
    sizes = sizes.at[1:1 + 2 * pairs:2].set(giver - shifted).at[2:2 + 2 * pairs:2].set(sink + shifted)
    return sizes[jax.random.permutation(jax.random.fold_in(own_key, 2), number_of)]


def centred(key, extent, deviation, bound, pieces=(), kind=jnp.bfloat16):
    array = jax.random.normal(key, extent, jnp.float32) * deviation
    if len(pieces) > 0:
        array = block_levels(key, extent, pieces, -0.22, 0.18) * array
    return jnp.clip(array, min=-bound, max=bound).astype(kind)


def setup_inputs(seed: int = 0, part: int = 0) -> dict:
    keys = jax.random.split(jax.random.key(seed), 7)
    own_keys = jax.random.split(jax.random.fold_in(keys[6], part), 7)
    layer_input = draw_layer_input(jax.random.fold_in(jax.random.fold_in(keys[6], part), 71), part)
    query_weight = centred(keys[1], (D, HQ * DH), D ** -0.5, 0.09375, ((0, 4), (1, 4)))
    key_weight = centred(keys[2], (D, HK * DH), D ** -0.5, 0.09375, ((0, 4), (1, 4)))
    value_weight = centred(keys[3], (D, HK * DH), D ** -0.5, 0.09375, ((0, 4), (1, 4)))
    out_grad = centred(own_keys[4], (TOKENS, HQ * DH), 1.0, 6.0, ((0, 4), (1, 4)))
    doc_ids = jnp.searchsorted(jnp.cumsum(uneven_parts(own_keys[5], DOCS, TOKENS, MAXDOC, 2)), jnp.arange(TOKENS), side="right").astype(jnp.int32)
    return dict(layer_input=layer_input, query_weight=query_weight, key_weight=key_weight, value_weight=value_weight, out_grad=out_grad, doc_ids=doc_ids)


NEGATIVE = -1e30


def reference(layer_input, query_weight, key_weight, value_weight, out_grad, doc_ids):
    total_rows = layer_input.shape[0]
    group_size = HQ // HK
    factor_scale = DH ** -0.5
    queries = jnp.dot(layer_input, query_weight, preferred_element_type=jnp.float32).astype(jnp.bfloat16).reshape(total_rows, HQ, DH)
    keys_all = jnp.dot(layer_input, key_weight, preferred_element_type=jnp.float32).astype(jnp.bfloat16).reshape(total_rows, HK, DH)
    values_all = jnp.dot(layer_input, value_weight, preferred_element_type=jnp.float32).astype(jnp.bfloat16).reshape(total_rows, HK, DH)
    cotangent = out_grad.reshape(total_rows, HQ, DH)
    positions = jnp.arange(total_rows, dtype=jnp.int32)
    allowed = (doc_ids[None, :] == doc_ids[:, None]) & (positions[None, :] <= positions[:, None])

    def one_head(head_id):
        pair_id = head_id // group_size
        query_rows = lax.dynamic_index_in_dim(queries, head_id, 1, keepdims=False)
        key_rows = lax.dynamic_index_in_dim(keys_all, pair_id, 1, keepdims=False)
        value_rows = lax.dynamic_index_in_dim(values_all, pair_id, 1, keepdims=False)
        grad_rows = lax.dynamic_index_in_dim(cotangent, head_id, 1, keepdims=False)
        logits = jnp.dot(query_rows, key_rows.T, preferred_element_type=jnp.float32) * factor_scale
        logits = jnp.where(allowed, logits, NEGATIVE)
        weights = jnp.where(allowed, jnp.exp(logits - jnp.max(logits, axis=1, keepdims=True)), 0.0)
        attention = weights / jnp.sum(weights, axis=1, keepdims=True)
        slopes = jnp.dot(grad_rows, value_rows.T, preferred_element_type=jnp.float32)
        inner_sum = jnp.sum(attention * slopes, axis=1, keepdims=True)
        score_grad = (attention * (slopes - inner_sum) * factor_scale).astype(jnp.bfloat16)
        value_grad = jnp.dot(attention.astype(jnp.bfloat16).T, grad_rows, preferred_element_type=jnp.float32)
        key_grad = jnp.dot(score_grad.T, query_rows, preferred_element_type=jnp.float32)
        query_grad = jnp.dot(score_grad, key_rows, preferred_element_type=jnp.float32)
        return query_grad, key_grad, value_grad

    query_grad, key_grad, value_grad = lax.map(one_head, jnp.arange(HQ, dtype=jnp.int32))
    query_grad = jnp.transpose(query_grad.astype(jnp.bfloat16), (1, 0, 2)).reshape(total_rows, HQ * DH)
    key_grad = jnp.sum(key_grad.reshape(HK, group_size, total_rows, DH), axis=1).astype(jnp.bfloat16)
    key_grad = jnp.transpose(key_grad, (1, 0, 2)).reshape(total_rows, HK * DH)
    value_grad = jnp.sum(value_grad.reshape(HK, group_size, total_rows, DH), axis=1).astype(jnp.bfloat16)
    value_grad = jnp.transpose(value_grad, (1, 0, 2)).reshape(total_rows, HK * DH)
    input_grad = jnp.dot(query_grad, query_weight.T, preferred_element_type=jnp.float32)
    input_grad = input_grad + jnp.dot(key_grad, key_weight.T, preferred_element_type=jnp.float32)
    input_grad = input_grad + jnp.dot(value_grad, value_weight.T, preferred_element_type=jnp.float32)
    query_weight_grad = jnp.dot(layer_input.T, query_grad, preferred_element_type=jnp.float32)
    key_weight_grad = jnp.dot(layer_input.T, key_grad, preferred_element_type=jnp.float32)
    value_weight_grad = jnp.dot(layer_input.T, value_grad, preferred_element_type=jnp.float32)
    return input_grad.astype(jnp.bfloat16), query_weight_grad, key_weight_grad, value_weight_grad
```

```python
import functools

import jax
import jax.numpy as jnp
from jax import lax
from jax.experimental import pallas as pl
from jax.experimental.pallas import tpu as pltpu
from jax.sharding import PartitionSpec as P

HQ = 32
HK = 8
DH = 128
BLOCK = 128


NEGATIVE = -1e30


def attend(queries, cotangent, keys_all, values_all, doc_ids, block_id, carried):
    row_count = queries.shape[0]
    factor_scale = queries.shape[-1] ** (-0.5)
    offsets = jnp.arange(row_count, dtype=jnp.int32)
    query_pos = block_id * row_count + offsets
    query_doc = lax.dynamic_slice_in_dim(doc_ids, block_id * row_count, row_count)
    doc_start = jnp.sum((doc_ids < query_doc[0]).astype(jnp.int32))
    lowest = doc_start // row_count
    highest = jnp.where(True, block_id + 1, lowest)

    def scores_at(key_block):
        key_rows = lax.dynamic_slice_in_dim(keys_all, key_block * row_count, row_count, 0)
        value_rows = lax.dynamic_slice_in_dim(values_all, key_block * row_count, row_count, 0)
        key_doc = lax.dynamic_slice_in_dim(doc_ids, key_block * row_count, row_count)
        key_pos = key_block * row_count + offsets
        allowed = (key_doc[None, :] == query_doc[:, None]) & (
            key_pos[None, :] <= query_pos[:, None]
        )
        logits = (
            jnp.einsum("qgnd,kgd->gnqk", queries, key_rows, preferred_element_type=jnp.float32)
            * factor_scale
        )
        logits = jnp.where(allowed, logits, NEGATIVE)
        slopes = jnp.einsum(
            "qgnd,kgd->gnqk", cotangent, value_rows, preferred_element_type=jnp.float32
        )
        return (key_rows, allowed, logits, slopes)

    def first_pass(key_block, loop_state):
        row_peak, row_total, row_inner = loop_state
        key_rows, allowed, logits, slopes = scores_at(key_block)
        new_peak = jnp.maximum(row_peak, jnp.max(logits, axis=-1))
        weights = jnp.where(allowed, jnp.exp(logits - new_peak[..., None]), 0.0)
        factor = jnp.exp(row_peak - new_peak)
        row_total = row_total * factor + jnp.sum(weights, axis=-1)
        row_inner = row_inner * factor + jnp.sum(weights * slopes, axis=-1)
        return (new_peak, row_total, row_inner)

    stat_shape = (queries.shape[1], queries.shape[2], row_count)
    initial = (
        jnp.full(stat_shape, NEGATIVE, jnp.float32),
        jnp.zeros(stat_shape, jnp.float32),
        jnp.zeros(stat_shape, jnp.float32),
    )
    row_peak, row_total, row_inner = lax.fori_loop(lowest, highest, first_pass, initial)
    safe_total = jnp.where(True, row_total, 1.0)
    row_delta = row_inner / safe_total
    log_total = row_peak + jnp.log(safe_total)

    def second_pass(key_block, loop_state):
        query_grad, key_accum, value_accum = loop_state
        key_rows, allowed, logits, slopes = scores_at(key_block)
        attention = jnp.where(allowed, jnp.exp(logits - log_total[..., None]), 0.0)
        score_grad = (attention * (slopes - row_delta[..., None]) * factor_scale).astype(
            jnp.bfloat16
        )
        value_part = jnp.einsum(
            "gnqk,qgnd->kgd",
            attention.astype(jnp.bfloat16),
            cotangent,
            preferred_element_type=jnp.float32,
        )
        key_part = jnp.einsum(
            "gnqk,qgnd->kgd", score_grad, queries, preferred_element_type=jnp.float32
        )
        query_grad = query_grad + jnp.einsum(
            "gnqk,kgd->qgnd", score_grad, key_rows, preferred_element_type=jnp.float32
        )
        first_row = key_block * row_count
        key_accum = lax.dynamic_update_slice_in_dim(
            key_accum,
            lax.dynamic_slice_in_dim(key_accum, first_row, row_count, 0) + key_part,
            first_row,
            0,
        )
        value_accum = lax.dynamic_update_slice_in_dim(
            value_accum,
            lax.dynamic_slice_in_dim(value_accum, first_row, row_count, 0) + value_part,
            first_row,
            0,
        )
        return (query_grad, key_accum, value_accum)

    start_grad = jnp.zeros(queries.shape, jnp.float32)
    query_grad, key_accum, value_accum = lax.fori_loop(
        lowest, highest, second_pass, (start_grad, carried[0], carried[1])
    )
    return (query_grad, (key_accum, value_accum))


def body(layer_input, query_weight, key_weight, value_weight, out_grad, doc_ids):
    tok_rows = layer_input.shape[0]
    query_width = query_weight.shape[1]
    pair_width = key_weight.shape[1]
    key_heads = pair_width // DH
    group_size = HQ // HK
    block_count = tok_rows // BLOCK
    owner_id = lax.axis_index("srv")
    weights_all = lax.all_gather(
        jnp.concatenate([query_weight, key_weight, value_weight], axis=1), "srv", axis=0, tiled=True
    )
    inputs_all = lax.all_gather(layer_input, ("hid", "rep"), axis=1, tiled=True)
    projected = jnp.dot(inputs_all, weights_all, preferred_element_type=jnp.float32).astype(
        jnp.bfloat16
    )
    queries = projected[:, :query_width].reshape(block_count, BLOCK, key_heads, group_size, DH)
    keys_local = projected[:, query_width : query_width + pair_width]
    values_local = projected[:, query_width + pair_width :]
    keys_all, values_all = (
        lax.all_gather(keys_local, "srv", axis=0, tiled=True),
        lax.all_gather(values_local, "srv", axis=0, tiled=True),
    )
    total_rows = keys_all.shape[0]
    keys_all = keys_all.reshape(total_rows, key_heads, DH)
    values_all = values_all.reshape(total_rows, key_heads, DH)
    cotangent = out_grad.reshape(block_count, BLOCK, key_heads, group_size, DH)
    empty_accum = jnp.zeros((total_rows, key_heads, DH), jnp.float32)

    def own_block(position, loop_state):
        answers, carried = loop_state
        grad_q, carried = attend(
            lax.dynamic_index_in_dim(queries, position, 0, keepdims=False),
            lax.dynamic_index_in_dim(cotangent, position, 0, keepdims=False),
            keys_all,
            values_all,
            doc_ids,
            owner_id * block_count + position,
            carried,
        )
        answers = lax.dynamic_update_index_in_dim(answers, grad_q.astype(jnp.bfloat16), position, 0)
        return (answers, carried)

    answers = jnp.zeros(queries.shape, jnp.bfloat16)
    answers, carried = lax.fori_loop(
        0, block_count, own_block, (answers, (empty_accum, empty_accum))
    )
    query_grad = answers.reshape(tok_rows, query_width)
    key_accum, value_accum = carried
    key_sum, value_sum = (
        lax.psum_scatter(key_accum, "srv", scatter_dimension=0, tiled=True),
        lax.psum_scatter(value_accum, "srv", scatter_dimension=0, tiled=True),
    )
    grads_all = jnp.concatenate(
        [
            query_grad,
            key_sum.astype(jnp.bfloat16).reshape(tok_rows, pair_width),
            value_sum.astype(jnp.bfloat16).reshape(tok_rows, pair_width),
        ],
        axis=1,
    )
    input_terms = lax.dot_general(
        grads_all, weights_all, (((1,), (1,)), ((), ())), preferred_element_type=jnp.float32
    )
    input_grad = lax.psum_scatter(
        input_terms, ("hid", "rep"), scatter_dimension=1, tiled=True
    ).astype(jnp.bfloat16)
    columns = lax.all_to_all(inputs_all, "srv", split_axis=1, concat_axis=0, tiled=True)
    weight_grad = lax.dot_general(
        columns,
        lax.all_gather(grads_all, "srv", axis=0, tiled=True),
        (((0,), (0,)), ((), ())),
        preferred_element_type=jnp.float32,
    )
    return (
        input_grad,
        weight_grad[:, :query_width],
        weight_grad[:, query_width : query_width + pair_width],
        weight_grad[:, query_width + pair_width :],
    )


MESH = pl.DeviceIdType.MESH
VM = pl.BlockSpec(memory_space=pltpu.VMEM)
VMEM_BYTES = 60 * 1024 * 1024


def place(n_rep):
    return lax.axis_index("srv"), lax.axis_index("hid") * n_rep + lax.axis_index("rep")


def device_at(z, c, n_rep):
    return {"srv": z, "hid": c // n_rep, "rep": c % n_rep}


def greet(n, m, n_rep):
    z, c = place(n_rep)
    barrier = pltpu.get_barrier_semaphore()
    for dz in range(n):
        for dc in range(m):
            if dz or dc:
                pl.semaphore_signal(
                    barrier,
                    inc=1,
                    device_id=device_at((z + dz) % n, (c + dc) % m, n_rep),
                    device_id_type=MESH,
                )
    pl.semaphore_wait(barrier, n * m - 1)


def remote(src, dst, send, recv, device):
    return pltpu.make_async_remote_copy(
        src_ref=src, dst_ref=dst, send_sem=send, recv_sem=recv, device_id=device, device_id_type=MESH
    )


def rows_at(start, size):
    return pl.ds(pl.multiple_of(start, size), size)


def project_kernel(
    n, m, n_rep, share,
    x_ref, og_ref, qw_ref, kw_ref, vw_ref,
    cols_ref, og_out, qkv_ref,
    part, took,
    og_send, og_recv, a_send, a_recv, b_send, b_recv, c_send, c_recv, own_sem,
):
    z, c = place(n_rep)
    tok = x_ref.shape[0]
    piece = tok // m
    q_cols = qw_ref.shape[1] // n
    greet(n, m, n_rep)

    own = c == z
    for dq in range(m):
        q = (c + dq) % m
        src = x_ref.at[rows_at(q * piece, piece)]
        dst = cols_ref.at[rows_at(z * tok + q * piece, piece)]
        if dq == 0:
            @pl.when(own)
            def _():
                pltpu.make_async_copy(src, dst, a_recv.at[z]).start()

            @pl.when(jnp.logical_not(own))
            def _():
                remote(src, dst, a_send.at[dq], a_recv.at[z], device_at(c, q, n_rep)).start()
        else:
            remote(src, dst, a_send.at[dq], a_recv.at[z], device_at(c, q, n_rep)).start()
    og_dst = og_out.at[rows_at(z * tok, tok)]
    og_copies = []
    for d in range(1, n):
        to = (z + d) % n
        copy = remote(
            og_ref.at[:, rows_at(to * q_cols, q_cols)], og_dst,
            og_send.at[d], og_recv.at[d], device_at(to, c, n_rep),
        )
        copy.start()
        og_copies.append(copy)
    og_own = pltpu.make_async_copy(og_ref.at[:, rows_at(z * q_cols, q_cols)], og_dst, own_sem)
    og_own.start()

    def spread_copy(t, d):
        block = cols_ref.at[rows_at(t * tok + c * piece, piece)]
        return remote(
            block, block, b_send.at[t, d], b_recv.at[t, d], device_at(z, (c + d) % m, n_rep)
        )

    def part_copy(t, d):
        to = (z + d) % n
        rows = rows_at(t * tok, tok)
        return remote(
            part.at[to, rows], took.at[d - 1, rows],
            c_send.at[t, d], c_recv.at[t, d], device_at(to, c, n_rep),
        )

    def spread(i, carry):
        t = (z + i) % n
        block = cols_ref.at[rows_at(t * tok + c * piece, piece)]
        pltpu.make_async_copy(block, block, a_recv.at[t]).wait()
        for d in range(1, m):
            spread_copy(t, d).start()
        return carry

    lax.fori_loop(0, n, spread, 0)

    def multiply(i, carry):
        t = (z + i) % n
        for d in range(1, m):
            spread_copy(t, d).wait_recv()
        rows = rows_at(t * tok, tok)
        x = cols_ref[rows, :]
        keys = jnp.dot(x, kw_ref[...], preferred_element_type=jnp.float32).astype(jnp.bfloat16)
        values = jnp.dot(x, vw_ref[...], preferred_element_type=jnp.float32).astype(jnp.bfloat16)
        for s in range(n):
            j = s // share
            part[s, rows, :q_cols] = jnp.dot(
                x, qw_ref[:, s * q_cols : (s + 1) * q_cols], preferred_element_type=jnp.float32
            ).astype(jnp.bfloat16)
            part[s, rows, q_cols : q_cols + DH] = keys[:, j * DH : (j + 1) * DH]
            part[s, rows, q_cols + DH :] = values[:, j * DH : (j + 1) * DH]
        for d in range(1, n):
            part_copy(t, d).start()
        return carry

    lax.fori_loop(0, n, multiply, 0)

    def collect(i, carry):
        t = (z + i) % n
        rows = rows_at(t * tok, tok)
        for d in range(1, n):
            part_copy(t, d).wait_recv()
        total = part[z, rows, :].astype(jnp.float32)
        for d in range(1, n):
            total = total + took[d - 1, rows, :].astype(jnp.float32)
        qkv_ref[rows, :] = total.astype(jnp.bfloat16)
        return carry

    lax.fori_loop(0, n, collect, 0)

    def drain(t, carry):
        for d in range(1, m):
            spread_copy(t, d).wait_send()
        for d in range(1, n):
            part_copy(t, d).wait_send()
        return carry

    lax.fori_loop(0, n, drain, 0)
    og_own.wait()
    for copy in og_copies:
        copy.wait()
    for dq in range(m):
        q = (c + dq) % m
        src = x_ref.at[rows_at(q * piece, piece)]
        dst = cols_ref.at[rows_at(z * tok + q * piece, piece)]
        copy = remote(src, dst, a_send.at[dq], a_recv.at[z], device_at(c, q, n_rep))
        if dq == 0:
            @pl.when(jnp.logical_not(own))
            def _():
                copy.wait_send()
        else:
            copy.wait_send()


def attend_kernel(longest, row_block, qkv_ref, og_ref, dr_ref, dc_ref, dq_ref, mine_ref, give_ref, dk, dv):
    total_rows = qkv_ref.shape[0]
    q_cols = og_ref.shape[1]
    heads = q_cols // DH
    scale = DH ** (-0.5)
    dk[...] = jnp.zeros_like(dk)
    dv[...] = jnp.zeros_like(dv)
    for first in range(0, total_rows, row_block):
        last = first + row_block
        low = max(0, (first + 1 - longest) // 128 * 128)
        width = last - low
        queries = jnp.concatenate(
            [qkv_ref[first:last, h * DH : (h + 1) * DH] for h in range(heads)], axis=0
        )
        cotangent = jnp.concatenate(
            [og_ref[first:last, h * DH : (h + 1) * DH] for h in range(heads)], axis=0
        )
        keys = qkv_ref[low:last, q_cols : q_cols + DH]
        values = qkv_ref[low:last, q_cols + DH :]
        row_pos = first + lax.broadcasted_iota(jnp.int32, (row_block, width), 0)
        key_pos = low + lax.broadcasted_iota(jnp.int32, (row_block, width), 1)
        kept = (dr_ref[first:last, :] == dc_ref[:, low:last]) & (key_pos <= row_pos)
        allowed = jnp.concatenate([jnp.where(kept, 1.0, 0.0)] * heads, axis=0) > 0.5
        both = (((1,), (1,)), ((), ()))
        logits = lax.dot_general(queries, keys, both, preferred_element_type=jnp.float32) * scale
        logits = jnp.where(allowed, logits, NEGATIVE)
        weights = jnp.where(allowed, jnp.exp(logits - jnp.max(logits, axis=1, keepdims=True)), 0.0)
        attention = weights / jnp.sum(weights, axis=1, keepdims=True)
        slopes = lax.dot_general(cotangent, values, both, preferred_element_type=jnp.float32)
        inner = jnp.sum(attention * slopes, axis=1, keepdims=True)
        score_grad = (attention * (slopes - inner) * scale).astype(jnp.bfloat16)
        down = (((0,), (0,)), ((), ()))
        query_grad = jnp.dot(score_grad, keys, preferred_element_type=jnp.float32)
        for h in range(heads):
            dq_ref[first:last, h * DH : (h + 1) * DH] = query_grad[
                h * row_block : (h + 1) * row_block
            ].astype(jnp.bfloat16)
        dk[low:last, :] += lax.dot_general(
            score_grad, queries, down, preferred_element_type=jnp.float32
        )
        dv[low:last, :] += lax.dot_general(
            attention.astype(jnp.bfloat16), cotangent, down, preferred_element_type=jnp.float32
        )
    odd = lax.axis_index("srv") % 2 == 1

    @pl.when(odd)
    def _():
        mine_ref[...] = dv[...]
        give_ref[...] = dk[...].astype(jnp.bfloat16)

    @pl.when(jnp.logical_not(odd))
    def _():
        mine_ref[...] = dk[...]
        give_ref[...] = dv[...].astype(jnp.bfloat16)


def spread_kernel(
    n, m, n_rep,
    dq_ref, mine_ref, give_ref, qw_ref, kw_ref, vw_ref,
    dqa_ref, kva_ref, ig_ref,
    pair, stage, terms, took, done,
    p_send, p_recv, q_send, q_recv, k_send, k_recv, r_send, r_recv, e_send, e_recv,
):
    z, c = place(n_rep)
    tok, _ = ig_ref.shape
    piece = tok // m
    q_cols = dq_ref.shape[1]
    greet(n, m, n_rep)
    odd = z % 2
    pair_copy = remote(
        give_ref, pair, p_send, p_recv, device_at(z + 1 - 2 * odd, c, n_rep)
    )
    pair_copy.start()
    my_cols = rows_at(z * q_cols, q_cols)
    my_head = rows_at((z // 2) * DH, DH)

    def query_copy(t, d):
        rows = rows_at(t * tok, tok)
        return remote(
            dq_ref.at[rows], dqa_ref.at[rows, my_cols],
            q_send.at[t, d], q_recv.at[t, d], device_at((z + d) % n, c, n_rep),
        )

    def pair_out(t, d):
        rows = rows_at(t * tok, tok)
        return remote(
            stage.at[rows], kva_ref.at[odd, rows, my_head],
            k_send.at[t, d], k_recv.at[t, d], device_at((z + d) % n, c, n_rep),
        )

    def term_copy(t, d):
        to = (c + d) % m
        return remote(
            terms.at[rows_at(t * tok + to * piece, piece)],
            took.at[d - 1, rows_at(t * piece, piece)],
            r_send.at[t, d], r_recv.at[t, d], device_at(z, to, n_rep),
        )

    def done_copy(t):
        return remote(
            done.at[rows_at(t * piece, piece)], ig_ref.at[rows_at(c * piece, piece)],
            e_send.at[t], e_recv.at[c], device_at(t, z, n_rep),
        )

    for d in range(1, n):
        query_copy(0, d).start()
    dqa_ref[:, my_cols] = dq_ref[...]
    pair_copy.wait()
    summed = (mine_ref[...] + pair[...].astype(jnp.float32)).astype(jnp.bfloat16)
    stage[...] = summed
    kva_ref[odd, :, my_head] = summed
    for d in range(1, n):
        pair_out(0, d).start()

    def send_chunk(t, carry):
        for d in range(1, n):
            query_copy(t, d).start()
        for d in range(1, n):
            pair_out(t, d).start()
        return carry

    lax.fori_loop(1, n, send_chunk, 0)

    def finish(t):
        for d in range(1, m):
            term_copy(t, d).wait_recv()
        total = terms[rows_at(t * tok + c * piece, piece), :].astype(jnp.float32)
        for d in range(1, m):
            total = total + took[d - 1, rows_at(t * piece, piece), :].astype(jnp.float32)
        done[rows_at(t * piece, piece), :] = total.astype(jnp.bfloat16)
        own = (t == z) & (c == z)

        @pl.when(own)
        def _():
            pltpu.make_async_copy(
                done.at[rows_at(t * piece, piece)],
                ig_ref.at[rows_at(c * piece, piece)],
                e_recv.at[c],
            ).start()

        @pl.when(jnp.logical_not(own))
        def _():
            done_copy(t).start()

    def chunk(t, carry):
        rows = rows_at(t * tok, tok)
        for d in range(1, n):
            query_copy(t, d).wait_recv()
            pair_out(t, d).wait_recv()
        across = (((1,), (1,)), ((), ()))
        total = lax.dot_general(
            dqa_ref[rows, :], qw_ref[...], across, preferred_element_type=jnp.float32
        )
        total = total + lax.dot_general(
            kva_ref[0, rows, :], kw_ref[...], across, preferred_element_type=jnp.float32
        )
        total = total + lax.dot_general(
            kva_ref[1, rows, :], vw_ref[...], across, preferred_element_type=jnp.float32
        )
        terms[rows, :] = total.astype(jnp.bfloat16)
        for d in range(1, m):
            term_copy(t, d).start()

        @pl.when(t > 0)
        def _():
            finish(t - 1)

        return carry

    lax.fori_loop(0, n, chunk, 0)
    finish(jnp.int32(n - 1))

    def drain(t, carry):
        for d in range(1, n):
            query_copy(t, d).wait_send()
            pair_out(t, d).wait_send()
        for d in range(1, m):
            term_copy(t, d).wait_send()

        @pl.when(jnp.logical_not((t == z) & (c == z)))
        def _():
            done_copy(t).wait_send()

        return carry

    lax.fori_loop(0, n, drain, 0)
    for q in range(m):
        block = ig_ref.at[q * piece : (q + 1) * piece]
        pltpu.make_async_copy(block, block, e_recv.at[q]).wait()


def stationary(n, n_hid, n_rep, layer_input, query_weight, key_weight, value_weight, out_grad, doc_ids):
    m = n_hid * n_rep
    bf16, f32 = jnp.bfloat16, jnp.float32
    tok, feats = layer_input.shape
    total = tok * n
    q_cols = query_weight.shape[1] // n
    pair_width = key_weight.shape[1]
    share = n // (pair_width // DH)
    width = q_cols + 2 * DH
    dma = pltpu.SemaphoreType.DMA
    columns, cotangent, qkv = pl.pallas_call(
        functools.partial(project_kernel, n, m, n_rep, share),
        out_shape=(
            jax.ShapeDtypeStruct((total, feats), bf16),
            jax.ShapeDtypeStruct((total, q_cols), bf16),
            jax.ShapeDtypeStruct((total, width), bf16),
        ),
        in_specs=[VM] * 5,
        out_specs=(VM,) * 3,
        scratch_shapes=[
            pltpu.VMEM((n, total, width), bf16),
            pltpu.VMEM((n - 1, total, width), bf16),
            dma((n,)), dma((n,)), dma((m,)), dma((n,)),
            dma((n, m)), dma((n, m)), dma((n, n)), dma((n, n)), dma,
        ],
        compiler_params=pltpu.CompilerParams(
            collective_id=0, has_side_effects=True, vmem_limit_bytes=VMEM_BYTES
        ),
    )(layer_input, out_grad, query_weight, key_weight, value_weight)
    query_grad, mine, give = pl.pallas_call(
        functools.partial(attend_kernel, total // 2, BLOCK),
        out_shape=(
            jax.ShapeDtypeStruct((total, q_cols), bf16),
            jax.ShapeDtypeStruct((total, DH), f32),
            jax.ShapeDtypeStruct((total, DH), bf16),
        ),
        in_specs=[VM] * 4,
        out_specs=(VM,) * 3,
        scratch_shapes=[pltpu.VMEM((total, DH), f32), pltpu.VMEM((total, DH), f32)],
        compiler_params=pltpu.CompilerParams(vmem_limit_bytes=VMEM_BYTES),
    )(qkv, cotangent, doc_ids.reshape(total, 1), doc_ids.reshape(1, total))
    queries_all, pairs_all, input_grad = pl.pallas_call(
        functools.partial(spread_kernel, n, m, n_rep),
        out_shape=(
            jax.ShapeDtypeStruct((total, q_cols * n), bf16),
            jax.ShapeDtypeStruct((2, total, pair_width), bf16),
            jax.ShapeDtypeStruct((tok, feats), bf16),
        ),
        in_specs=[VM] * 6,
        out_specs=(VM,) * 3,
        scratch_shapes=[
            pltpu.VMEM((total, DH), bf16),
            pltpu.VMEM((total, DH), bf16),
            pltpu.VMEM((total, feats), bf16),
            pltpu.VMEM((m - 1, tok // m * n, feats), bf16),
            pltpu.VMEM((tok // m * n, feats), bf16),
            dma, dma, dma((n, n)), dma((n, n)), dma((n, n)), dma((n, n)),
            dma((n, m)), dma((n, m)), dma((n,)), dma((m,)),
        ],
        compiler_params=pltpu.CompilerParams(
            collective_id=1, has_side_effects=True, vmem_limit_bytes=VMEM_BYTES
        ),
    )(query_grad, mine, give, query_weight, key_weight, value_weight)

    def weight_grad(grads):
        return lax.dot_general(
            columns, grads, (((0,), (0,)), ((), ())), preferred_element_type=f32
        )

    return (
        input_grad,
        weight_grad(queries_all),
        weight_grad(pairs_all[0]),
        weight_grad(pairs_all[1]),
    )


def solution(mesh):
    in_specs = (
        P(("groups", "srv"), ("hid", "rep")),
        P("srv", ("hid", "rep")),
        P("srv", ("hid", "rep")),
        P("srv", ("hid", "rep")),
        P(("groups", "srv"), ("hid", "rep")),
        P("groups"),
    )
    out_specs = (
        P(("groups", "srv"), ("hid", "rep")),
        P(("groups", "srv"), ("hid", "rep")),
        P(("groups", "srv"), ("hid", "rep")),
        P(("groups", "srv"), ("hid", "rep")),
    )
    n, n_hid, n_rep = mesh.shape["srv"], mesh.shape["hid"], mesh.shape["rep"]
    m = n_hid * n_rep
    inner = body
    if n == m and HK % m == 0 and 2 * (HK // m) == n and (HQ // m) % n == 0:
        inner = functools.partial(stationary, n, n_hid, n_rep)
    return jax.shard_map(inner, mesh=mesh, in_specs=in_specs, out_specs=out_specs, check_vma=False)
```

```python
import functools

import jax
import jax.numpy as jnp
from jax import lax
from jax.experimental import pallas as pl
from jax.experimental.pallas import tpu as pltpu
from jax.sharding import PartitionSpec as P

HQ = 32
HK = 8
DH = 128
BLOCK = 128


NEGATIVE = -1e30


def attend(queries, cotangent, keys_all, values_all, doc_ids, block_id, carried):
    row_count = queries.shape[0]
    factor_scale = queries.shape[-1] ** (-0.5)
    offsets = jnp.arange(row_count, dtype=jnp.int32)
    query_pos = block_id * row_count + offsets
    query_doc = lax.dynamic_slice_in_dim(doc_ids, block_id * row_count, row_count)
    doc_start = jnp.sum((doc_ids < query_doc[0]).astype(jnp.int32))
    lowest = doc_start // row_count
    highest = jnp.where(True, block_id + 1, lowest)

    def scores_at(key_block):
        key_rows = lax.dynamic_slice_in_dim(keys_all, key_block * row_count, row_count, 0)
        value_rows = lax.dynamic_slice_in_dim(values_all, key_block * row_count, row_count, 0)
        key_doc = lax.dynamic_slice_in_dim(doc_ids, key_block * row_count, row_count)
        key_pos = key_block * row_count + offsets
        allowed = (key_doc[None, :] == query_doc[:, None]) & (
            key_pos[None, :] <= query_pos[:, None]
        )
        logits = (
            jnp.einsum("qgnd,kgd->gnqk", queries, key_rows, preferred_element_type=jnp.float32)
            * factor_scale
        )
        logits = jnp.where(allowed, logits, NEGATIVE)
        slopes = jnp.einsum(
            "qgnd,kgd->gnqk", cotangent, value_rows, preferred_element_type=jnp.float32
        )
        return (key_rows, allowed, logits, slopes)

    def first_pass(key_block, loop_state):
        row_peak, row_total, row_inner = loop_state
        key_rows, allowed, logits, slopes = scores_at(key_block)
        new_peak = jnp.maximum(row_peak, jnp.max(logits, axis=-1))
        weights = jnp.where(allowed, jnp.exp(logits - new_peak[..., None]), 0.0)
        factor = jnp.exp(row_peak - new_peak)
        row_total = row_total * factor + jnp.sum(weights, axis=-1)
        row_inner = row_inner * factor + jnp.sum(weights * slopes, axis=-1)
        return (new_peak, row_total, row_inner)

    stat_shape = (queries.shape[1], queries.shape[2], row_count)
    initial = (
        jnp.full(stat_shape, NEGATIVE, jnp.float32),
        jnp.zeros(stat_shape, jnp.float32),
        jnp.zeros(stat_shape, jnp.float32),
    )
    row_peak, row_total, row_inner = lax.fori_loop(lowest, highest, first_pass, initial)
    safe_total = jnp.where(True, row_total, 1.0)
    row_delta = row_inner / safe_total
    log_total = row_peak + jnp.log(safe_total)

    def second_pass(key_block, loop_state):
        query_grad, key_accum, value_accum = loop_state
        key_rows, allowed, logits, slopes = scores_at(key_block)
        attention = jnp.where(allowed, jnp.exp(logits - log_total[..., None]), 0.0)
        score_grad = (attention * (slopes - row_delta[..., None]) * factor_scale).astype(
            jnp.bfloat16
        )
        value_part = jnp.einsum(
            "gnqk,qgnd->kgd",
            attention.astype(jnp.bfloat16),
            cotangent,
            preferred_element_type=jnp.float32,
        )
        key_part = jnp.einsum(
            "gnqk,qgnd->kgd", score_grad, queries, preferred_element_type=jnp.float32
        )
        query_grad = query_grad + jnp.einsum(
            "gnqk,kgd->qgnd", score_grad, key_rows, preferred_element_type=jnp.float32
        )
        first_row = key_block * row_count
        key_accum = lax.dynamic_update_slice_in_dim(
            key_accum,
            lax.dynamic_slice_in_dim(key_accum, first_row, row_count, 0) + key_part,
            first_row,
            0,
        )
        value_accum = lax.dynamic_update_slice_in_dim(
            value_accum,
            lax.dynamic_slice_in_dim(value_accum, first_row, row_count, 0) + value_part,
            first_row,
            0,
        )
        return (query_grad, key_accum, value_accum)

    start_grad = jnp.zeros(queries.shape, jnp.float32)
    query_grad, key_accum, value_accum = lax.fori_loop(
        lowest, highest, second_pass, (start_grad, carried[0], carried[1])
    )
    return (query_grad, (key_accum, value_accum))


def body(layer_input, query_weight, key_weight, value_weight, out_grad, doc_ids):
    tok_rows = layer_input.shape[0]
    query_width = query_weight.shape[1]
    pair_width = key_weight.shape[1]
    key_heads = pair_width // DH
    group_size = HQ // HK
    block_count = tok_rows // BLOCK
    owner_id = lax.axis_index("srv")
    weights_all = lax.all_gather(
        jnp.concatenate([query_weight, key_weight, value_weight], axis=1), "srv", axis=0, tiled=True
    )
    inputs_all = lax.all_gather(layer_input, ("hid", "rep"), axis=1, tiled=True)
    projected = jnp.dot(inputs_all, weights_all, preferred_element_type=jnp.float32).astype(
        jnp.bfloat16
    )
    queries = projected[:, :query_width].reshape(block_count, BLOCK, key_heads, group_size, DH)
    keys_local = projected[:, query_width : query_width + pair_width]
    values_local = projected[:, query_width + pair_width :]
    keys_all, values_all = (
        lax.all_gather(keys_local, "srv", axis=0, tiled=True),
        lax.all_gather(values_local, "srv", axis=0, tiled=True),
    )
    total_rows = keys_all.shape[0]
    keys_all = keys_all.reshape(total_rows, key_heads, DH)
    values_all = values_all.reshape(total_rows, key_heads, DH)
    cotangent = out_grad.reshape(block_count, BLOCK, key_heads, group_size, DH)
    empty_accum = jnp.zeros((total_rows, key_heads, DH), jnp.float32)

    def own_block(position, loop_state):
        answers, carried = loop_state
        grad_q, carried = attend(
            lax.dynamic_index_in_dim(queries, position, 0, keepdims=False),
            lax.dynamic_index_in_dim(cotangent, position, 0, keepdims=False),
            keys_all,
            values_all,
            doc_ids,
            owner_id * block_count + position,
            carried,
        )
        answers = lax.dynamic_update_index_in_dim(answers, grad_q.astype(jnp.bfloat16), position, 0)
        return (answers, carried)

    answers = jnp.zeros(queries.shape, jnp.bfloat16)
    answers, carried = lax.fori_loop(
        0, block_count, own_block, (answers, (empty_accum, empty_accum))
    )
    query_grad = answers.reshape(tok_rows, query_width)
    key_accum, value_accum = carried
    key_sum, value_sum = (
        lax.psum_scatter(key_accum, "srv", scatter_dimension=0, tiled=True),
        lax.psum_scatter(value_accum, "srv", scatter_dimension=0, tiled=True),
    )
    grads_all = jnp.concatenate(
        [
            query_grad,
            key_sum.astype(jnp.bfloat16).reshape(tok_rows, pair_width),
            value_sum.astype(jnp.bfloat16).reshape(tok_rows, pair_width),
        ],
        axis=1,
    )
    input_terms = lax.dot_general(
        grads_all, weights_all, (((1,), (1,)), ((), ())), preferred_element_type=jnp.float32
    )
    input_grad = lax.psum_scatter(
        input_terms, ("hid", "rep"), scatter_dimension=1, tiled=True
    ).astype(jnp.bfloat16)
    columns = lax.all_to_all(inputs_all, "srv", split_axis=1, concat_axis=0, tiled=True)
    weight_grad = lax.dot_general(
        columns,
        lax.all_gather(grads_all, "srv", axis=0, tiled=True),
        (((0,), (0,)), ((), ())),
        preferred_element_type=jnp.float32,
    )
    return (
        input_grad,
        weight_grad[:, :query_width],
        weight_grad[:, query_width : query_width + pair_width],
        weight_grad[:, query_width + pair_width :],
    )


MESH = pl.DeviceIdType.MESH
VM = pl.BlockSpec(memory_space=pltpu.VMEM)
VMEM_BYTES = 60 * 1024 * 1024


def place(n_rep):
    return lax.axis_index("srv"), lax.axis_index("hid") * n_rep + lax.axis_index("rep")


def device_at(z, c, n_rep):
    return {"srv": z, "hid": c // n_rep, "rep": c % n_rep}


def greet(n, m, n_rep):
    z, c = place(n_rep)
    barrier = pltpu.get_barrier_semaphore()
    for dz in range(n):
        for dc in range(m):
            if dz or dc:
                pl.semaphore_signal(
                    barrier,
                    inc=1,
                    device_id=device_at((z + dz) % n, (c + dc) % m, n_rep),
                    device_id_type=MESH,
                )
    pl.semaphore_wait(barrier, n * m - 1)


def remote(src, dst, send, recv, device):
    return pltpu.make_async_remote_copy(
        src_ref=src, dst_ref=dst, send_sem=send, recv_sem=recv, device_id=device, device_id_type=MESH
    )


def rows_at(start, size):
    return pl.ds(pl.multiple_of(start, size), size)


def project_kernel(
    n, m, n_rep, share,
    x_ref, og_ref, qw_ref, kw_ref, vw_ref,
    cols_ref, og_out, qkv_ref,
    part, took, relay,
    og_send, og_recv, a_send, a_recv, b_send, b_recv, c_send, c_recv, v_send, v_recv, own_sem,
):
    z, c = place(n_rep)
    tok = x_ref.shape[0]
    piece = tok // m
    q_cols = qw_ref.shape[1] // n
    half, odd = z // 2, z % 2
    partner = z + 1 - 2 * odd
    middle = half != odd
    far = 2 * (1 - half)
    kv_cols = rows_at(q_cols + odd * DH, DH)
    greet(n, m, n_rep)

    own = c == z
    for dq in range(m):
        q = (c + dq) % m
        src = x_ref.at[rows_at(q * piece, piece)]
        dst = cols_ref.at[rows_at(z * tok + q * piece, piece)]
        if dq == 0:
            @pl.when(own)
            def _():
                pltpu.make_async_copy(src, dst, a_recv.at[z]).start()

            @pl.when(jnp.logical_not(own))
            def _():
                remote(src, dst, a_send.at[dq], a_recv.at[z], device_at(c, q, n_rep)).start()
        else:
            remote(src, dst, a_send.at[dq], a_recv.at[z], device_at(c, q, n_rep)).start()
    og_dst = og_out.at[rows_at(z * tok, tok)]
    og_copies = []
    for d in range(1, n):
        to = (z + d) % n
        copy = remote(
            og_ref.at[:, rows_at(to * q_cols, q_cols)], og_dst,
            og_send.at[d], og_recv.at[d], device_at(to, c, n_rep),
        )
        copy.start()
        og_copies.append(copy)
    og_own = pltpu.make_async_copy(og_ref.at[:, rows_at(z * q_cols, q_cols)], og_dst, own_sem)
    og_own.start()

    def spread_copy(t, d):
        block = cols_ref.at[rows_at(t * tok + c * piece, piece)]
        return remote(
            block, block, b_send.at[t, d], b_recv.at[t, d], device_at(z, (c + d) % m, n_rep)
        )

    def part_copy(t, slot):
        rows = rows_at(t * tok, tok)
        src = part.at[partner if slot == 0 else far + slot - 1, rows]
        dst = took.at[0, rows] if slot == 0 else relay.at[slot - 1, rows]
        return remote(
            src, dst, c_send.at[t, slot], c_recv.at[t, slot], device_at(partner, c, n_rep)
        )

    def far_copy(t, slot):
        to = far + slot - 1
        rows = rows_at(t * tok, tok)
        return remote(
            part.at[to, rows], took.at[1, rows],
            c_send.at[t, slot], c_recv.at[t, 3], device_at(to, c, n_rep),
        )

    def swap_copy(t):
        block = qkv_ref.at[rows_at(t * tok, tok), kv_cols]
        return remote(block, block, v_send.at[t], v_recv.at[t], device_at(partner, c, n_rep))

    def pass_on(t):
        rows = rows_at(t * tok, tok)

        @pl.when(middle)
        def _():
            for slot in (1, 2):
                part_copy(t, slot).wait_recv()
                to = far + slot - 1
                total = part[to, rows, :].astype(jnp.float32)
                total = total + relay[slot - 1, rows, :].astype(jnp.float32)
                part[to, rows, :] = total.astype(jnp.bfloat16)
                far_copy(t, slot).start()

    def spread(i, carry):
        t = (2 * half + i) % n
        block = cols_ref.at[rows_at(t * tok + c * piece, piece)]
        pltpu.make_async_copy(block, block, a_recv.at[t]).wait()
        for d in range(1, m):
            spread_copy(t, d).start()
        return carry

    lax.fori_loop(0, n, spread, 0)

    def multiply(i, carry):
        t = (2 * half + i) % n
        for d in range(1, m):
            spread_copy(t, d).wait_recv()
        rows = rows_at(t * tok, tok)
        x = cols_ref[rows, :]
        keys = jnp.dot(x, kw_ref[...], preferred_element_type=jnp.float32).astype(jnp.bfloat16)
        values = jnp.dot(x, vw_ref[...], preferred_element_type=jnp.float32).astype(jnp.bfloat16)
        for s in range(n):
            j = s // share
            part[s, rows, :q_cols] = jnp.dot(
                x, qw_ref[:, s * q_cols : (s + 1) * q_cols], preferred_element_type=jnp.float32
            ).astype(jnp.bfloat16)
            pair = values if s % 2 else keys
            part[s, rows, q_cols:] = pair[:, j * DH : (j + 1) * DH]

        @pl.when(jnp.logical_not(middle))
        def _():
            for slot in (1, 2):
                part_copy(t, slot).start()

        part_copy(t, 0).start()

        @pl.when(i > 0)
        def _():
            pass_on((2 * half + i - 1) % n)

        return carry

    lax.fori_loop(0, n, multiply, 0)
    pass_on((2 * half + n - 1) % n)

    def collect(i, carry):
        t = (2 * half + i) % n
        rows = rows_at(t * tok, tok)
        part_copy(t, 0).wait_recv()
        pltpu.make_async_copy(took.at[1, rows], took.at[1, rows], c_recv.at[t, 3]).wait()
        total = part[z, rows, :].astype(jnp.float32)
        for slot in range(2):
            total = total + took[slot, rows, :].astype(jnp.float32)
        total = total.astype(jnp.bfloat16)
        qkv_ref[rows, :q_cols] = total[:, :q_cols]
        qkv_ref[rows, kv_cols] = total[:, q_cols:]
        swap_copy(t).start()
        return carry

    lax.fori_loop(0, n, collect, 0)

    def drain(t, carry):
        for d in range(1, m):
            spread_copy(t, d).wait_send()
        for slot in range(3):
            part_copy(t, slot).wait_send()
        swap_copy(t).wait()
        return carry

    lax.fori_loop(0, n, drain, 0)
    og_own.wait()
    for copy in og_copies:
        copy.wait()
    for dq in range(m):
        q = (c + dq) % m
        src = x_ref.at[rows_at(q * piece, piece)]
        dst = cols_ref.at[rows_at(z * tok + q * piece, piece)]
        copy = remote(src, dst, a_send.at[dq], a_recv.at[z], device_at(c, q, n_rep))
        if dq == 0:
            @pl.when(jnp.logical_not(own))
            def _():
                copy.wait_send()
        else:
            copy.wait_send()


def attend_kernel(longest, row_block, qkv_ref, og_ref, dr_ref, dc_ref, dq_ref, mine_ref, give_ref, dk, dv):
    total_rows = qkv_ref.shape[0]
    q_cols = og_ref.shape[1]
    heads = q_cols // DH
    scale = DH ** (-0.5)
    dk[...] = jnp.zeros_like(dk)
    dv[...] = jnp.zeros_like(dv)
    for first in range(0, total_rows, row_block):
        last = first + row_block
        low = max(0, (first + 1 - longest) // 128 * 128)
        width = last - low
        queries = jnp.concatenate(
            [qkv_ref[first:last, h * DH : (h + 1) * DH] for h in range(heads)], axis=0
        )
        cotangent = jnp.concatenate(
            [og_ref[first:last, h * DH : (h + 1) * DH] for h in range(heads)], axis=0
        )
        keys = qkv_ref[low:last, q_cols : q_cols + DH]
        values = qkv_ref[low:last, q_cols + DH :]
        row_pos = first + lax.broadcasted_iota(jnp.int32, (row_block, width), 0)
        key_pos = low + lax.broadcasted_iota(jnp.int32, (row_block, width), 1)
        kept = (dr_ref[first:last, :] == dc_ref[:, low:last]) & (key_pos <= row_pos)
        allowed = jnp.concatenate([jnp.where(kept, 1.0, 0.0)] * heads, axis=0) > 0.5
        both = (((1,), (1,)), ((), ()))
        logits = lax.dot_general(queries, keys, both, preferred_element_type=jnp.float32) * scale
        logits = jnp.where(allowed, logits, NEGATIVE)
        weights = jnp.where(allowed, jnp.exp(logits - jnp.max(logits, axis=1, keepdims=True)), 0.0)
        attention = weights / jnp.sum(weights, axis=1, keepdims=True)
        slopes = lax.dot_general(cotangent, values, both, preferred_element_type=jnp.float32)
        inner = jnp.sum(attention * slopes, axis=1, keepdims=True)
        score_grad = (attention * (slopes - inner) * scale).astype(jnp.bfloat16)
        down = (((0,), (0,)), ((), ()))
        query_grad = jnp.dot(score_grad, keys, preferred_element_type=jnp.float32)
        for h in range(heads):
            dq_ref[first:last, h * DH : (h + 1) * DH] = query_grad[
                h * row_block : (h + 1) * row_block
            ].astype(jnp.bfloat16)
        dk[low:last, :] += lax.dot_general(
            score_grad, queries, down, preferred_element_type=jnp.float32
        )
        dv[low:last, :] += lax.dot_general(
            attention.astype(jnp.bfloat16), cotangent, down, preferred_element_type=jnp.float32
        )
    odd = lax.axis_index("srv") % 2 == 1

    @pl.when(odd)
    def _():
        mine_ref[...] = dv[...]
        give_ref[...] = dk[...].astype(jnp.bfloat16)

    @pl.when(jnp.logical_not(odd))
    def _():
        mine_ref[...] = dk[...]
        give_ref[...] = dv[...].astype(jnp.bfloat16)


def spread_kernel(
    n, m, n_rep,
    dq_ref, mine_ref, give_ref, qw_ref, kw_ref, vw_ref,
    dqa_ref, kva_ref, ig_ref,
    pair, stage, terms, took, done,
    p_send, p_recv, q_send, q_recv, k_send, k_recv, r_send, r_recv, e_send, e_recv,
):
    z, c = place(n_rep)
    tok, _ = ig_ref.shape
    piece = tok // m
    q_cols = dq_ref.shape[1]
    greet(n, m, n_rep)
    half, odd = z // 2, z % 2
    partner = z + 1 - 2 * odd
    middle = half != odd
    far = 2 * (1 - half)
    near = 2 - half
    pair_copy = remote(give_ref, pair, p_send, p_recv, device_at(partner, c, n_rep))
    pair_copy.start()
    my_cols = rows_at(z * q_cols, q_cols)
    my_head = rows_at(half * DH, DH)

    def query_copy(t, slot):
        rows = rows_at(t * tok, tok)
        owner = z if slot < 2 else far + slot - 2
        there = dqa_ref.at[rows, rows_at(owner * q_cols, q_cols)]
        return remote(
            dq_ref.at[rows] if slot < 2 else there, there,
            q_send.at[t, slot], q_recv.at[t, owner],
            device_at(near if slot == 1 else partner, c, n_rep),
        )

    def pair_out(t, slot):
        rows = rows_at(t * tok, tok)
        owner = z if slot < 2 else far + slot - 2
        there = kva_ref.at[owner % 2, rows, rows_at(owner // 2 * DH, DH)]
        return remote(
            stage.at[rows] if slot < 2 else there, there,
            k_send.at[t, slot], k_recv.at[t, owner],
            device_at(near if slot == 1 else partner, c, n_rep),
        )

    def await_owner(t, owner):
        rows = rows_at(t * tok, tok)
        block = dqa_ref.at[rows, rows_at(owner * q_cols, q_cols)]
        pltpu.make_async_copy(block, block, q_recv.at[t, owner]).wait()

    def await_pair(t, owner):
        rows = rows_at(t * tok, tok)
        block = kva_ref.at[owner % 2, rows, rows_at(owner // 2 * DH, DH)]
        pltpu.make_async_copy(block, block, k_recv.at[t, owner]).wait()

    def term_copy(t, d):
        to = (c + d) % m
        return remote(
            terms.at[rows_at(t * tok + to * piece, piece)],
            took.at[d - 1, rows_at(t * piece, piece)],
            r_send.at[t, d], r_recv.at[t, d], device_at(z, to, n_rep),
        )

    def done_copy(t):
        return remote(
            done.at[rows_at(t * piece, piece)], ig_ref.at[rows_at(c * piece, piece)],
            e_send.at[t], e_recv.at[c], device_at(t, z, n_rep),
        )

    for slot in (1, 0):
        query_copy(0, slot).start()
    dqa_ref[:, my_cols] = dq_ref[...]
    pair_copy.wait()
    summed = (mine_ref[...] + pair[...].astype(jnp.float32)).astype(jnp.bfloat16)
    stage[...] = summed
    kva_ref[odd, :, my_head] = summed
    for slot in (1, 0):
        pair_out(0, slot).start()

    def send_chunk(t, carry):
        for slot in (1, 0):
            query_copy(t, slot).start()
            pair_out(t, slot).start()
        return carry

    lax.fori_loop(1, n, send_chunk, 0)

    def finish(t):
        for d in range(1, m):
            term_copy(t, d).wait_recv()
        total = terms[rows_at(t * tok + c * piece, piece), :].astype(jnp.float32)
        for d in range(1, m):
            total = total + took[d - 1, rows_at(t * piece, piece), :].astype(jnp.float32)
        done[rows_at(t * piece, piece), :] = total.astype(jnp.bfloat16)
        own = (t == z) & (c == z)

        @pl.when(own)
        def _():
            pltpu.make_async_copy(
                done.at[rows_at(t * piece, piece)],
                ig_ref.at[rows_at(c * piece, piece)],
                e_recv.at[c],
            ).start()

        @pl.when(jnp.logical_not(own))
        def _():
            done_copy(t).start()

    def chunk(t, carry):
        rows = rows_at(t * tok, tok)
        for slot in (2, 3):
            await_owner(t, far + slot - 2)

            @pl.when(middle)
            def _():
                query_copy(t, slot).start()

        for slot in (2, 3):
            await_pair(t, far + slot - 2)

            @pl.when(middle)
            def _():
                pair_out(t, slot).start()

        await_owner(t, partner)
        await_pair(t, partner)
        across = (((1,), (1,)), ((), ()))
        total = lax.dot_general(
            dqa_ref[rows, :], qw_ref[...], across, preferred_element_type=jnp.float32
        )
        total = total + lax.dot_general(
            kva_ref[0, rows, :], kw_ref[...], across, preferred_element_type=jnp.float32
        )
        total = total + lax.dot_general(
            kva_ref[1, rows, :], vw_ref[...], across, preferred_element_type=jnp.float32
        )
        terms[rows, :] = total.astype(jnp.bfloat16)
        for d in range(1, m):
            term_copy(t, d).start()

        @pl.when(t > 0)
        def _():
            finish(t - 1)

        return carry

    lax.fori_loop(0, n, chunk, 0)
    finish(jnp.int32(n - 1))

    def drain(t, carry):
        for slot in (0, 1):
            query_copy(t, slot).wait_send()
            pair_out(t, slot).wait_send()

        @pl.when(middle)
        def _():
            for slot in (2, 3):
                query_copy(t, slot).wait_send()
                pair_out(t, slot).wait_send()

        for d in range(1, m):
            term_copy(t, d).wait_send()

        @pl.when(jnp.logical_not((t == z) & (c == z)))
        def _():
            done_copy(t).wait_send()

        return carry

    lax.fori_loop(0, n, drain, 0)
    for q in range(m):
        block = ig_ref.at[q * piece : (q + 1) * piece]
        pltpu.make_async_copy(block, block, e_recv.at[q]).wait()


def stationary(n, n_hid, n_rep, layer_input, query_weight, key_weight, value_weight, out_grad, doc_ids):
    m = n_hid * n_rep
    bf16, f32 = jnp.bfloat16, jnp.float32
    tok, feats = layer_input.shape
    total = tok * n
    q_cols = query_weight.shape[1] // n
    pair_width = key_weight.shape[1]
    share = n // (pair_width // DH)
    width = q_cols + 2 * DH
    dma = pltpu.SemaphoreType.DMA
    columns, cotangent, qkv = pl.pallas_call(
        functools.partial(project_kernel, n, m, n_rep, share),
        out_shape=(
            jax.ShapeDtypeStruct((total, feats), bf16),
            jax.ShapeDtypeStruct((total, q_cols), bf16),
            jax.ShapeDtypeStruct((total, width), bf16),
        ),
        in_specs=[VM] * 5,
        out_specs=(VM,) * 3,
        scratch_shapes=[
            pltpu.VMEM((n, total, q_cols + DH), bf16),
            pltpu.VMEM((2, total, q_cols + DH), bf16),
            pltpu.VMEM((2, total, q_cols + DH), bf16),
            dma((n,)), dma((n,)), dma((m,)), dma((n,)),
            dma((n, m)), dma((n, m)), dma((n, 3)), dma((n, 4)), dma((n,)), dma((n,)), dma,
        ],
        compiler_params=pltpu.CompilerParams(
            collective_id=0, has_side_effects=True, vmem_limit_bytes=VMEM_BYTES
        ),
    )(layer_input, out_grad, query_weight, key_weight, value_weight)
    query_grad, mine, give = pl.pallas_call(
        functools.partial(attend_kernel, total // 2, BLOCK),
        out_shape=(
            jax.ShapeDtypeStruct((total, q_cols), bf16),
            jax.ShapeDtypeStruct((total, DH), f32),
            jax.ShapeDtypeStruct((total, DH), bf16),
        ),
        in_specs=[VM] * 4,
        out_specs=(VM,) * 3,
        scratch_shapes=[pltpu.VMEM((total, DH), f32), pltpu.VMEM((total, DH), f32)],
        compiler_params=pltpu.CompilerParams(vmem_limit_bytes=VMEM_BYTES),
    )(qkv, cotangent, doc_ids.reshape(total, 1), doc_ids.reshape(1, total))
    queries_all, pairs_all, input_grad = pl.pallas_call(
        functools.partial(spread_kernel, n, m, n_rep),
        out_shape=(
            jax.ShapeDtypeStruct((total, q_cols * n), bf16),
            jax.ShapeDtypeStruct((2, total, pair_width), bf16),
            jax.ShapeDtypeStruct((tok, feats), bf16),
        ),
        in_specs=[VM] * 6,
        out_specs=(VM,) * 3,
        scratch_shapes=[
            pltpu.VMEM((total, DH), bf16),
            pltpu.VMEM((total, DH), bf16),
            pltpu.VMEM((total, feats), bf16),
            pltpu.VMEM((m - 1, tok // m * n, feats), bf16),
            pltpu.VMEM((tok // m * n, feats), bf16),
            dma, dma, dma((n, n)), dma((n, n)), dma((n, n)), dma((n, n)),
            dma((n, m)), dma((n, m)), dma((n,)), dma((m,)),
        ],
        compiler_params=pltpu.CompilerParams(
            collective_id=1, has_side_effects=True, vmem_limit_bytes=VMEM_BYTES
        ),
    )(query_grad, mine, give, query_weight, key_weight, value_weight)

    def weight_grad(grads):
        return lax.dot_general(
            columns, grads, (((0,), (0,)), ((), ())), preferred_element_type=f32
        )

    return (
        input_grad,
        weight_grad(queries_all),
        weight_grad(pairs_all[0]),
        weight_grad(pairs_all[1]),
    )


def solution(mesh):
    in_specs = (
        P(("groups", "srv"), ("hid", "rep")),
        P("srv", ("hid", "rep")),
        P("srv", ("hid", "rep")),
        P("srv", ("hid", "rep")),
        P(("groups", "srv"), ("hid", "rep")),
        P("groups"),
    )
    out_specs = (
        P(("groups", "srv"), ("hid", "rep")),
        P(("groups", "srv"), ("hid", "rep")),
        P(("groups", "srv"), ("hid", "rep")),
        P(("groups", "srv"), ("hid", "rep")),
    )
    n, n_hid, n_rep = mesh.shape["srv"], mesh.shape["hid"], mesh.shape["rep"]
    m = n_hid * n_rep
    inner = body
    if n == m and HK % m == 0 and 2 * (HK // m) == n and (HQ // m) % n == 0:
        inner = functools.partial(stationary, n, n_hid, n_rep)
    return jax.shard_map(inner, mesh=mesh, in_specs=in_specs, out_specs=out_specs, check_vma=False)
```

```python
import functools

import jax
import jax.numpy as jnp
from jax import lax
from jax.experimental import pallas as pl
from jax.experimental.pallas import tpu as pltpu
from jax.sharding import PartitionSpec as P

HQ = 32
HK = 8
DH = 128
BLOCK = 128


NEGATIVE = -1e30


def attend(queries, cotangent, keys_all, values_all, doc_ids, block_id, carried):
    row_count = queries.shape[0]
    factor_scale = queries.shape[-1] ** (-0.5)
    offsets = jnp.arange(row_count, dtype=jnp.int32)
    query_pos = block_id * row_count + offsets
    query_doc = lax.dynamic_slice_in_dim(doc_ids, block_id * row_count, row_count)
    doc_start = jnp.sum((doc_ids < query_doc[0]).astype(jnp.int32))
    lowest = doc_start // row_count
    highest = jnp.where(True, block_id + 1, lowest)

    def scores_at(key_block):
        key_rows = lax.dynamic_slice_in_dim(keys_all, key_block * row_count, row_count, 0)
        value_rows = lax.dynamic_slice_in_dim(values_all, key_block * row_count, row_count, 0)
        key_doc = lax.dynamic_slice_in_dim(doc_ids, key_block * row_count, row_count)
        key_pos = key_block * row_count + offsets
        allowed = (key_doc[None, :] == query_doc[:, None]) & (
            key_pos[None, :] <= query_pos[:, None]
        )
        logits = (
            jnp.einsum("qgnd,kgd->gnqk", queries, key_rows, preferred_element_type=jnp.float32)
            * factor_scale
        )
        logits = jnp.where(allowed, logits, NEGATIVE)
        slopes = jnp.einsum(
            "qgnd,kgd->gnqk", cotangent, value_rows, preferred_element_type=jnp.float32
        )
        return (key_rows, allowed, logits, slopes)

    def first_pass(key_block, loop_state):
        row_peak, row_total, row_inner = loop_state
        key_rows, allowed, logits, slopes = scores_at(key_block)
        new_peak = jnp.maximum(row_peak, jnp.max(logits, axis=-1))
        weights = jnp.where(allowed, jnp.exp(logits - new_peak[..., None]), 0.0)
        factor = jnp.exp(row_peak - new_peak)
        row_total = row_total * factor + jnp.sum(weights, axis=-1)
        row_inner = row_inner * factor + jnp.sum(weights * slopes, axis=-1)
        return (new_peak, row_total, row_inner)

    stat_shape = (queries.shape[1], queries.shape[2], row_count)
    initial = (
        jnp.full(stat_shape, NEGATIVE, jnp.float32),
        jnp.zeros(stat_shape, jnp.float32),
        jnp.zeros(stat_shape, jnp.float32),
    )
    row_peak, row_total, row_inner = lax.fori_loop(lowest, highest, first_pass, initial)
    safe_total = jnp.where(True, row_total, 1.0)
    row_delta = row_inner / safe_total
    log_total = row_peak + jnp.log(safe_total)

    def second_pass(key_block, loop_state):
        query_grad, key_accum, value_accum = loop_state
        key_rows, allowed, logits, slopes = scores_at(key_block)
        attention = jnp.where(allowed, jnp.exp(logits - log_total[..., None]), 0.0)
        score_grad = (attention * (slopes - row_delta[..., None]) * factor_scale).astype(
            jnp.bfloat16
        )
        value_part = jnp.einsum(
            "gnqk,qgnd->kgd",
            attention.astype(jnp.bfloat16),
            cotangent,
            preferred_element_type=jnp.float32,
        )
        key_part = jnp.einsum(
            "gnqk,qgnd->kgd", score_grad, queries, preferred_element_type=jnp.float32
        )
        query_grad = query_grad + jnp.einsum(
            "gnqk,kgd->qgnd", score_grad, key_rows, preferred_element_type=jnp.float32
        )
        first_row = key_block * row_count
        key_accum = lax.dynamic_update_slice_in_dim(
            key_accum,
            lax.dynamic_slice_in_dim(key_accum, first_row, row_count, 0) + key_part,
            first_row,
            0,
        )
        value_accum = lax.dynamic_update_slice_in_dim(
            value_accum,
            lax.dynamic_slice_in_dim(value_accum, first_row, row_count, 0) + value_part,
            first_row,
            0,
        )
        return (query_grad, key_accum, value_accum)

    start_grad = jnp.zeros(queries.shape, jnp.float32)
    query_grad, key_accum, value_accum = lax.fori_loop(
        lowest, highest, second_pass, (start_grad, carried[0], carried[1])
    )
    return (query_grad, (key_accum, value_accum))


def body(layer_input, query_weight, key_weight, value_weight, out_grad, doc_ids):
    tok_rows = layer_input.shape[0]
    query_width = query_weight.shape[1]
    pair_width = key_weight.shape[1]
    key_heads = pair_width // DH
    group_size = HQ // HK
    block_count = tok_rows // BLOCK
    owner_id = lax.axis_index("srv")
    weights_all = lax.all_gather(
        jnp.concatenate([query_weight, key_weight, value_weight], axis=1), "srv", axis=0, tiled=True
    )
    inputs_all = lax.all_gather(layer_input, ("hid", "rep"), axis=1, tiled=True)
    projected = jnp.dot(inputs_all, weights_all, preferred_element_type=jnp.float32).astype(
        jnp.bfloat16
    )
    queries = projected[:, :query_width].reshape(block_count, BLOCK, key_heads, group_size, DH)
    keys_local = projected[:, query_width : query_width + pair_width]
    values_local = projected[:, query_width + pair_width :]
    keys_all, values_all = (
        lax.all_gather(keys_local, "srv", axis=0, tiled=True),
        lax.all_gather(values_local, "srv", axis=0, tiled=True),
    )
    total_rows = keys_all.shape[0]
    keys_all = keys_all.reshape(total_rows, key_heads, DH)
    values_all = values_all.reshape(total_rows, key_heads, DH)
    cotangent = out_grad.reshape(block_count, BLOCK, key_heads, group_size, DH)
    empty_accum = jnp.zeros((total_rows, key_heads, DH), jnp.float32)

    def own_block(position, loop_state):
        answers, carried = loop_state
        grad_q, carried = attend(
            lax.dynamic_index_in_dim(queries, position, 0, keepdims=False),
            lax.dynamic_index_in_dim(cotangent, position, 0, keepdims=False),
            keys_all,
            values_all,
            doc_ids,
            owner_id * block_count + position,
            carried,
        )
        answers = lax.dynamic_update_index_in_dim(answers, grad_q.astype(jnp.bfloat16), position, 0)
        return (answers, carried)

    answers = jnp.zeros(queries.shape, jnp.bfloat16)
    answers, carried = lax.fori_loop(
        0, block_count, own_block, (answers, (empty_accum, empty_accum))
    )
    query_grad = answers.reshape(tok_rows, query_width)
    key_accum, value_accum = carried
    key_sum, value_sum = (
        lax.psum_scatter(key_accum, "srv", scatter_dimension=0, tiled=True),
        lax.psum_scatter(value_accum, "srv", scatter_dimension=0, tiled=True),
    )
    grads_all = jnp.concatenate(
        [
            query_grad,
            key_sum.astype(jnp.bfloat16).reshape(tok_rows, pair_width),
            value_sum.astype(jnp.bfloat16).reshape(tok_rows, pair_width),
        ],
        axis=1,
    )
    input_terms = lax.dot_general(
        grads_all, weights_all, (((1,), (1,)), ((), ())), preferred_element_type=jnp.float32
    )
    input_grad = lax.psum_scatter(
        input_terms, ("hid", "rep"), scatter_dimension=1, tiled=True
    ).astype(jnp.bfloat16)
    columns = lax.all_to_all(inputs_all, "srv", split_axis=1, concat_axis=0, tiled=True)
    weight_grad = lax.dot_general(
        columns,
        lax.all_gather(grads_all, "srv", axis=0, tiled=True),
        (((0,), (0,)), ((), ())),
        preferred_element_type=jnp.float32,
    )
    return (
        input_grad,
        weight_grad[:, :query_width],
        weight_grad[:, query_width : query_width + pair_width],
        weight_grad[:, query_width + pair_width :],
    )


MESH = pl.DeviceIdType.MESH
VM = pl.BlockSpec(memory_space=pltpu.VMEM)
VMEM_BYTES = 60 * 1024 * 1024


def place(n_rep):
    return lax.axis_index("srv"), lax.axis_index("hid") * n_rep + lax.axis_index("rep")


def device_at(z, c, n_rep):
    return {"srv": z, "hid": c // n_rep, "rep": c % n_rep}


def greet(n, m, n_rep):
    z, c = place(n_rep)
    barrier = pltpu.get_barrier_semaphore()
    for dz in range(n):
        for dc in range(m):
            if dz or dc:
                pl.semaphore_signal(
                    barrier,
                    inc=1,
                    device_id=device_at((z + dz) % n, (c + dc) % m, n_rep),
                    device_id_type=MESH,
                )
    pl.semaphore_wait(barrier, n * m - 1)


def remote(src, dst, send, recv, device):
    return pltpu.make_async_remote_copy(
        src_ref=src, dst_ref=dst, send_sem=send, recv_sem=recv, device_id=device, device_id_type=MESH
    )


def rows_at(start, size):
    return pl.ds(pl.multiple_of(start, size), size)


def project_kernel(
    n, m, n_rep, share,
    x_ref, og_ref, qw_ref, kw_ref, vw_ref,
    cols_ref, og_out, qkv_ref,
    part, took, relay,
    og_send, og_recv, a_send, a_recv, b_send, b_recv, c_send, c_recv, v_send, v_recv, own_sem,
):
    z, c = place(n_rep)
    tok = x_ref.shape[0]
    piece = tok // m
    q_cols = qw_ref.shape[1] // n
    half, odd = z // 2, z % 2
    partner = z + 1 - 2 * odd
    middle = half != odd
    far = 2 * (1 - half)
    kv_cols = rows_at(q_cols + odd * DH, DH)
    greet(n, m, n_rep)

    own = c == z
    for dq in range(m):
        q = (c + dq) % m
        src = x_ref.at[rows_at(q * piece, piece)]
        dst = cols_ref.at[rows_at(z * tok + q * piece, piece)]
        if dq == 0:
            @pl.when(own)
            def _():
                pltpu.make_async_copy(src, dst, a_recv.at[z]).start()

            @pl.when(jnp.logical_not(own))
            def _():
                remote(src, dst, a_send.at[dq], a_recv.at[z], device_at(c, q, n_rep)).start()
        else:
            remote(src, dst, a_send.at[dq], a_recv.at[z], device_at(c, q, n_rep)).start()
    og_dst = og_out.at[rows_at(z * tok, tok)]
    og_copies = []
    for d in range(1, n):
        to = (z + d) % n
        copy = remote(
            og_ref.at[:, rows_at(to * q_cols, q_cols)], og_dst,
            og_send.at[d], og_recv.at[d], device_at(to, c, n_rep),
        )
        copy.start()
        og_copies.append(copy)
    og_own = pltpu.make_async_copy(og_ref.at[:, rows_at(z * q_cols, q_cols)], og_dst, own_sem)
    og_own.start()

    def spread_copy(t, d):
        block = cols_ref.at[rows_at(t * tok + c * piece, piece)]
        return remote(
            block, block, b_send.at[t, d], b_recv.at[t, d], device_at(z, (c + d) % m, n_rep)
        )

    def part_copy(t, slot):
        rows = rows_at(t * tok, tok)
        src = part.at[partner if slot == 0 else far + slot - 1, rows]
        dst = took.at[0, rows] if slot == 0 else relay.at[slot - 1, rows]
        return remote(
            src, dst, c_send.at[t, slot], c_recv.at[t, slot], device_at(partner, c, n_rep)
        )

    def far_copy(t, slot):
        to = far + slot - 1
        rows = rows_at(t * tok, tok)
        return remote(
            part.at[to, rows], took.at[1, rows],
            c_send.at[t, slot], c_recv.at[t, 3], device_at(to, c, n_rep),
        )

    def swap_copy(t):
        block = qkv_ref.at[rows_at(t * tok, tok), kv_cols]
        return remote(block, block, v_send.at[t], v_recv.at[t], device_at(partner, c, n_rep))

    def pass_on(t):
        rows = rows_at(t * tok, tok)

        @pl.when(middle)
        def _():
            for slot in (1, 2):
                part_copy(t, slot).wait_recv()
                to = far + slot - 1
                total = part[to, rows, :].astype(jnp.float32)
                total = total + relay[slot - 1, rows, :].astype(jnp.float32)
                part[to, rows, :] = total.astype(jnp.bfloat16)
                far_copy(t, slot).start()

    def spread(i, carry):
        t = (2 * half + i) % n
        block = cols_ref.at[rows_at(t * tok + c * piece, piece)]
        pltpu.make_async_copy(block, block, a_recv.at[t]).wait()
        for d in range(1, m):
            spread_copy(t, d).start()
        return carry

    lax.fori_loop(0, n, spread, 0)

    def multiply(i, carry):
        t = (2 * half + i) % n
        for d in range(1, m):
            spread_copy(t, d).wait_recv()
        rows = rows_at(t * tok, tok)
        x = cols_ref[rows, :]
        keys = jnp.dot(x, kw_ref[...], preferred_element_type=jnp.float32).astype(jnp.bfloat16)
        values = jnp.dot(x, vw_ref[...], preferred_element_type=jnp.float32).astype(jnp.bfloat16)
        for s in range(n):
            j = s // share
            part[s, rows, :q_cols] = jnp.dot(
                x, qw_ref[:, s * q_cols : (s + 1) * q_cols], preferred_element_type=jnp.float32
            ).astype(jnp.bfloat16)
            pair = values if s % 2 else keys
            part[s, rows, q_cols:] = pair[:, j * DH : (j + 1) * DH]

        @pl.when(jnp.logical_not(middle))
        def _():
            for slot in (1, 2):
                part_copy(t, slot).start()

        part_copy(t, 0).start()

        @pl.when(i > 0)
        def _():
            pass_on((2 * half + i - 1) % n)

        return carry

    lax.fori_loop(0, n, multiply, 0)
    pass_on((2 * half + n - 1) % n)

    def collect(i, carry):
        t = (2 * half + i) % n
        rows = rows_at(t * tok, tok)
        part_copy(t, 0).wait_recv()
        pltpu.make_async_copy(took.at[1, rows], took.at[1, rows], c_recv.at[t, 3]).wait()
        total = part[z, rows, :].astype(jnp.float32)
        for slot in range(2):
            total = total + took[slot, rows, :].astype(jnp.float32)
        total = total.astype(jnp.bfloat16)
        qkv_ref[rows, :q_cols] = total[:, :q_cols]
        qkv_ref[rows, kv_cols] = total[:, q_cols:]
        swap_copy(t).start()
        return carry

    lax.fori_loop(0, n, collect, 0)

    def drain(t, carry):
        for d in range(1, m):
            spread_copy(t, d).wait_send()
        for slot in range(3):
            part_copy(t, slot).wait_send()
        swap_copy(t).wait()
        return carry

    lax.fori_loop(0, n, drain, 0)
    og_own.wait()
    for copy in og_copies:
        copy.wait()
    for dq in range(m):
        q = (c + dq) % m
        src = x_ref.at[rows_at(q * piece, piece)]
        dst = cols_ref.at[rows_at(z * tok + q * piece, piece)]
        copy = remote(src, dst, a_send.at[dq], a_recv.at[z], device_at(c, q, n_rep))
        if dq == 0:
            @pl.when(jnp.logical_not(own))
            def _():
                copy.wait_send()
        else:
            copy.wait_send()


def attend_kernel(longest, row_block, qkv_ref, og_ref, dr_ref, dc_ref, dq_ref, mine_ref, give_ref, dk, dv):
    total_rows = qkv_ref.shape[0]
    q_cols = og_ref.shape[1]
    heads = q_cols // DH
    scale = DH ** (-0.5)
    dk[...] = jnp.zeros_like(dk)
    dv[...] = jnp.zeros_like(dv)
    for first in range(0, total_rows, row_block):
        last = first + row_block
        low = max(0, (first + 1 - longest) // 128 * 128)
        width = last - low
        queries = jnp.concatenate(
            [qkv_ref[first:last, h * DH : (h + 1) * DH] for h in range(heads)], axis=0
        )
        cotangent = jnp.concatenate(
            [og_ref[first:last, h * DH : (h + 1) * DH] for h in range(heads)], axis=0
        )
        keys = qkv_ref[low:last, q_cols : q_cols + DH]
        values = qkv_ref[low:last, q_cols + DH :]
        row_pos = first + lax.broadcasted_iota(jnp.int32, (row_block, width), 0)
        key_pos = low + lax.broadcasted_iota(jnp.int32, (row_block, width), 1)
        kept = (dr_ref[first:last, :] == dc_ref[:, low:last]) & (key_pos <= row_pos)
        allowed = jnp.concatenate([jnp.where(kept, 1.0, 0.0)] * heads, axis=0) > 0.5
        both = (((1,), (1,)), ((), ()))
        logits = lax.dot_general(queries, keys, both, preferred_element_type=jnp.float32) * scale
        logits = jnp.where(allowed, logits, NEGATIVE)
        weights = jnp.where(allowed, jnp.exp(logits - jnp.max(logits, axis=1, keepdims=True)), 0.0)
        attention = weights / jnp.sum(weights, axis=1, keepdims=True)
        slopes = lax.dot_general(cotangent, values, both, preferred_element_type=jnp.float32)
        inner = jnp.sum(attention * slopes, axis=1, keepdims=True)
        score_grad = (attention * (slopes - inner) * scale).astype(jnp.bfloat16)
        down = (((0,), (0,)), ((), ()))
        query_grad = jnp.dot(score_grad, keys, preferred_element_type=jnp.float32)
        for h in range(heads):
            dq_ref[first:last, h * DH : (h + 1) * DH] = query_grad[
                h * row_block : (h + 1) * row_block
            ].astype(jnp.bfloat16)
        dk[low:last, :] += lax.dot_general(
            score_grad, queries, down, preferred_element_type=jnp.float32
        )
        dv[low:last, :] += lax.dot_general(
            attention.astype(jnp.bfloat16), cotangent, down, preferred_element_type=jnp.float32
        )
    odd = lax.axis_index("srv") % 2 == 1

    @pl.when(odd)
    def _():
        mine_ref[...] = dv[...]
        give_ref[...] = dk[...].astype(jnp.bfloat16)

    @pl.when(jnp.logical_not(odd))
    def _():
        mine_ref[...] = dk[...]
        give_ref[...] = dv[...].astype(jnp.bfloat16)


def spread_kernel(
    n, m, n_rep,
    dq_ref, mine_ref, give_ref, qw_ref, kw_ref, vw_ref,
    dqa_ref, kva_ref, ig_ref,
    pair, stage, terms, took, done,
    p_send, p_recv, q_send, q_recv, k_send, k_recv, r_send, r_recv, e_send, e_recv,
):
    z, c = place(n_rep)
    tok, _ = ig_ref.shape
    piece = tok // m
    q_cols = dq_ref.shape[1]
    greet(n, m, n_rep)
    half, odd = z // 2, z % 2
    partner = z + 1 - 2 * odd
    middle = half != odd
    far = 2 * (1 - half)
    near = 2 - half
    pair_copy = remote(give_ref, pair, p_send, p_recv, device_at(partner, c, n_rep))
    pair_copy.start()
    my_cols = rows_at(z * q_cols, q_cols)
    my_head = rows_at(half * DH, DH)

    def query_copy(t, slot):
        rows = rows_at(t * tok, tok)
        owner = z if slot < 2 else far + slot - 2
        there = dqa_ref.at[rows, rows_at(owner * q_cols, q_cols)]
        return remote(
            dq_ref.at[rows] if slot < 2 else there, there,
            q_send.at[t, slot], q_recv.at[t, owner],
            device_at(near if slot == 1 else partner, c, n_rep),
        )

    def pair_out(t, slot):
        rows = rows_at(t * tok, tok)
        owner = z if slot < 2 else far + slot - 2
        there = kva_ref.at[owner % 2, rows, rows_at(owner // 2 * DH, DH)]
        return remote(
            stage.at[rows] if slot < 2 else there, there,
            k_send.at[t, slot], k_recv.at[t, owner],
            device_at(near if slot == 1 else partner, c, n_rep),
        )

    def await_owner(t, owner):
        rows = rows_at(t * tok, tok)
        block = dqa_ref.at[rows, rows_at(owner * q_cols, q_cols)]
        pltpu.make_async_copy(block, block, q_recv.at[t, owner]).wait()

    def await_pair(t, owner):
        rows = rows_at(t * tok, tok)
        block = kva_ref.at[owner % 2, rows, rows_at(owner // 2 * DH, DH)]
        pltpu.make_async_copy(block, block, k_recv.at[t, owner]).wait()

    def term_copy(t, d):
        to = (c + d) % m
        return remote(
            terms.at[rows_at(t * tok + to * piece, piece)],
            took.at[d - 1, rows_at(t * piece, piece)],
            r_send.at[t, d], r_recv.at[t, d], device_at(z, to, n_rep),
        )

    def done_copy(t):
        return remote(
            done.at[rows_at(t * piece, piece)], ig_ref.at[rows_at(c * piece, piece)],
            e_send.at[t], e_recv.at[c], device_at(t, z, n_rep),
        )

    for slot in (1, 0):
        query_copy(n - 1, slot).start()
    dqa_ref[:, my_cols] = dq_ref[...]
    pair_copy.wait()
    summed = (mine_ref[...] + pair[...].astype(jnp.float32)).astype(jnp.bfloat16)
    stage[...] = summed
    kva_ref[odd, :, my_head] = summed
    for slot in (1, 0):
        pair_out(n - 1, slot).start()

    def send_chunk(i, carry):
        t = (i + n - 1) % n
        for slot in (1, 0):
            query_copy(t, slot).start()
            pair_out(t, slot).start()
        return carry

    lax.fori_loop(1, n, send_chunk, 0)

    def finish(t):
        for d in range(1, m):
            term_copy(t, d).wait_recv()
        total = terms[rows_at(t * tok + c * piece, piece), :].astype(jnp.float32)
        for d in range(1, m):
            total = total + took[d - 1, rows_at(t * piece, piece), :].astype(jnp.float32)
        done[rows_at(t * piece, piece), :] = total.astype(jnp.bfloat16)
        own = (t == z) & (c == z)

        @pl.when(own)
        def _():
            pltpu.make_async_copy(
                done.at[rows_at(t * piece, piece)],
                ig_ref.at[rows_at(c * piece, piece)],
                e_recv.at[c],
            ).start()

        @pl.when(jnp.logical_not(own))
        def _():
            done_copy(t).start()

    def chunk(i, carry):
        t = (i + n - 1) % n
        rows = rows_at(t * tok, tok)
        for slot in (2, 3):
            await_owner(t, far + slot - 2)

            @pl.when(middle)
            def _():
                query_copy(t, slot).start()

        for slot in (2, 3):
            await_pair(t, far + slot - 2)

            @pl.when(middle)
            def _():
                pair_out(t, slot).start()

        await_owner(t, partner)
        await_pair(t, partner)
        across = (((1,), (1,)), ((), ()))
        total = lax.dot_general(
            dqa_ref[rows, :], qw_ref[...], across, preferred_element_type=jnp.float32
        )
        total = total + lax.dot_general(
            kva_ref[0, rows, :], kw_ref[...], across, preferred_element_type=jnp.float32
        )
        total = total + lax.dot_general(
            kva_ref[1, rows, :], vw_ref[...], across, preferred_element_type=jnp.float32
        )
        terms[rows, :] = total.astype(jnp.bfloat16)
        for d in range(1, m):
            term_copy(t, d).start()

        @pl.when(i > 0)
        def _():
            finish((i + n - 2) % n)

        return carry

    lax.fori_loop(0, n, chunk, 0)
    finish(jnp.int32(n - 2))

    def drain(t, carry):
        for slot in (0, 1):
            query_copy(t, slot).wait_send()
            pair_out(t, slot).wait_send()

        @pl.when(middle)
        def _():
            for slot in (2, 3):
                query_copy(t, slot).wait_send()
                pair_out(t, slot).wait_send()

        for d in range(1, m):
            term_copy(t, d).wait_send()

        @pl.when(jnp.logical_not((t == z) & (c == z)))
        def _():
            done_copy(t).wait_send()

        return carry

    lax.fori_loop(0, n, drain, 0)
    for q in range(m):
        block = ig_ref.at[q * piece : (q + 1) * piece]
        pltpu.make_async_copy(block, block, e_recv.at[q]).wait()


def stationary(n, n_hid, n_rep, layer_input, query_weight, key_weight, value_weight, out_grad, doc_ids):
    m = n_hid * n_rep
    bf16, f32 = jnp.bfloat16, jnp.float32
    tok, feats = layer_input.shape
    total = tok * n
    q_cols = query_weight.shape[1] // n
    pair_width = key_weight.shape[1]
    share = n // (pair_width // DH)
    width = q_cols + 2 * DH
    dma = pltpu.SemaphoreType.DMA
    columns, cotangent, qkv = pl.pallas_call(
        functools.partial(project_kernel, n, m, n_rep, share),
        out_shape=(
            jax.ShapeDtypeStruct((total, feats), bf16),
            jax.ShapeDtypeStruct((total, q_cols), bf16),
            jax.ShapeDtypeStruct((total, width), bf16),
        ),
        in_specs=[VM] * 5,
        out_specs=(VM,) * 3,
        scratch_shapes=[
            pltpu.VMEM((n, total, q_cols + DH), bf16),
            pltpu.VMEM((2, total, q_cols + DH), bf16),
            pltpu.VMEM((2, total, q_cols + DH), bf16),
            dma((n,)), dma((n,)), dma((m,)), dma((n,)),
            dma((n, m)), dma((n, m)), dma((n, 3)), dma((n, 4)), dma((n,)), dma((n,)), dma,
        ],
        compiler_params=pltpu.CompilerParams(
            collective_id=0, has_side_effects=True, vmem_limit_bytes=VMEM_BYTES
        ),
    )(layer_input, out_grad, query_weight, key_weight, value_weight)
    query_grad, mine, give = pl.pallas_call(
        functools.partial(attend_kernel, total // 2, BLOCK),
        out_shape=(
            jax.ShapeDtypeStruct((total, q_cols), bf16),
            jax.ShapeDtypeStruct((total, DH), f32),
            jax.ShapeDtypeStruct((total, DH), bf16),
        ),
        in_specs=[VM] * 4,
        out_specs=(VM,) * 3,
        scratch_shapes=[pltpu.VMEM((total, DH), f32), pltpu.VMEM((total, DH), f32)],
        compiler_params=pltpu.CompilerParams(vmem_limit_bytes=VMEM_BYTES),
    )(qkv, cotangent, doc_ids.reshape(total, 1), doc_ids.reshape(1, total))
    queries_all, pairs_all, input_grad = pl.pallas_call(
        functools.partial(spread_kernel, n, m, n_rep),
        out_shape=(
            jax.ShapeDtypeStruct((total, q_cols * n), bf16),
            jax.ShapeDtypeStruct((2, total, pair_width), bf16),
            jax.ShapeDtypeStruct((tok, feats), bf16),
        ),
        in_specs=[VM] * 6,
        out_specs=(VM,) * 3,
        scratch_shapes=[
            pltpu.VMEM((total, DH), bf16),
            pltpu.VMEM((total, DH), bf16),
            pltpu.VMEM((total, feats), bf16),
            pltpu.VMEM((m - 1, tok // m * n, feats), bf16),
            pltpu.VMEM((tok // m * n, feats), bf16),
            dma, dma, dma((n, n)), dma((n, n)), dma((n, n)), dma((n, n)),
            dma((n, m)), dma((n, m)), dma((n,)), dma((m,)),
        ],
        compiler_params=pltpu.CompilerParams(
            collective_id=1, has_side_effects=True, vmem_limit_bytes=VMEM_BYTES
        ),
    )(query_grad, mine, give, query_weight, key_weight, value_weight)

    def weight_grad(grads):
        return lax.dot_general(
            columns, grads, (((0,), (0,)), ((), ())), preferred_element_type=f32
        )

    return (
        input_grad,
        weight_grad(queries_all),
        weight_grad(pairs_all[0]),
        weight_grad(pairs_all[1]),
    )


def solution(mesh):
    in_specs = (
        P(("groups", "srv"), ("hid", "rep")),
        P("srv", ("hid", "rep")),
        P("srv", ("hid", "rep")),
        P("srv", ("hid", "rep")),
        P(("groups", "srv"), ("hid", "rep")),
        P("groups"),
    )
    out_specs = (
        P(("groups", "srv"), ("hid", "rep")),
        P(("groups", "srv"), ("hid", "rep")),
        P(("groups", "srv"), ("hid", "rep")),
        P(("groups", "srv"), ("hid", "rep")),
    )
    n, n_hid, n_rep = mesh.shape["srv"], mesh.shape["hid"], mesh.shape["rep"]
    m = n_hid * n_rep
    inner = body
    if n == m and HK % m == 0 and 2 * (HK // m) == n and (HQ // m) % n == 0:
        inner = functools.partial(stationary, n, n_hid, n_rep)
    return jax.shard_map(inner, mesh=mesh, in_specs=in_specs, out_specs=out_specs, check_vma=False)
```
